32 devices in a mesh: dp: 4 (over z), seq: 2 (over y), tensor: 4 (over x, core).
Axes of the slice: x: 2, y: 2, z: 4, core: 2. Of those that a mesh axis runs over, the one named last changes fastest.
Arguments:
- patch_states: bfloat16 [4, 768, 4096], P('dp', 'seq', 'tensor'), may hold values from -6 to 6
- residual_grad: bfloat16 [4, 768, 4096], P('dp', 'seq', 'tensor'), may hold values from -3 to 3
- upstream_value: bfloat16 [4, 768, 512], P('dp', 'seq'), may hold values from -6 to 6
- norm_gain: bfloat16 [4096], P('tensor'), may hold values from 0.099609375 to 1.8984375
- value_weight: bfloat16 [512, 4096], P(('dp', 'seq'), 'tensor'), may hold values from -0.09375 to 0.09375
- out_weight: bfloat16 [512, 4096], P(('dp', 'seq'), 'tensor'), may hold values from -0.25 to 0.25
- attn_out: bfloat16 [4, 768, 512], P('dp', 'seq'), may hold values from -6 to 6
- queries: bfloat16 [4, 768, 512], P('dp', 'seq', 'tensor'), may hold values from -1.5 to 1.5
- byte_keys: bfloat16 [4, 16384, 512], P('dp', 'seq', 'tensor'), may hold values from -1.5 to 1.5
- byte_values: bfloat16 [4, 16384, 512], P('dp', 'seq', 'tensor'), may hold values from -6 to 6
- patch_starts: int32 [4, 768], P('dp'), may hold values from 0 to 16383, as said below
Outputs:
- wgrad_value: float32 [512, 4096], P(('dp', 'seq'), 'tensor')
- wgrad_out: float32 [512, 4096], P(('dp', 'seq'), 'tensor')
- grad_keys: bfloat16 [4, 16384, 512], P('dp', 'seq', 'tensor')
- grad_values: bfloat16 [4, 16384, 512], P('dp', 'seq', 'tensor')
The draws below stay inside these ranges and needn't reach their ends.
Inputs may be any that keep to these rules, and one draw needn't show every extreme that they name: `patch_starts`: row i lists, increasing, the first byte of each of the 768 patches of sequence i. Every multiple of 8192 is among them, so no patch crosses the boundary between two byte shards. In every sequence one byte shard holds 768 patches, or 767 where that is fewer, and no byte shard holds more. The bytes of patch j lie on byte shard j // 384 - 1, j // 384 or j // 384 + 1.
All inputs are finite; a program needn't handle non-finite values.
Results may differ from the reference program's by a relative error of at most 0.0058.
Values may be sent and summed in bfloat16 or wider, within the bound.
A program may use at most 128 MiB of HBM per device.

```python
import math
import jax
import jax.numpy as jnp
from jax import lax

D = 4096
KVW = 512
DLW = 512
HD = 128
SEQ_LEN = 16384
PATCH_DEV = 384
SEQS = 4
NPS = 768
BYTE_DEV = 8192
N_SEQ = 2


def draw_patch_starts(key, part):

    def one_sequence(seq_key):
        heavy_key, weight_key, cut_key = jax.random.split(seq_key, 3)
        shard_ids = jnp.arange(N_SEQ, dtype=jnp.int32)
        heavy_shard = jax.random.randint(heavy_key, (), 0, N_SEQ)
        heavy_count = min(2 * PATCH_DEV, NPS - N_SEQ + 1)
        others_total = NPS - heavy_count
        short_total = (N_SEQ - 1) * PATCH_DEV - others_total
        others = (shard_ids != heavy_shard).astype(jnp.int32)
        weights = jax.random.randint(weight_key, (N_SEQ,), 1, 5) * others
        weight_total = jnp.sum(weights)
        shortfall = short_total * weights // weight_total
        deficit = short_total - jnp.sum(shortfall)
        ranking = jnp.cumsum(others) - 1
        shortfall = shortfall + ((ranking < deficit) & (others == 1)).astype(jnp.int32)
        counts = jnp.where(others == 1, PATCH_DEV - shortfall, heavy_count)
        cut_keys = jax.random.split(cut_key, N_SEQ)
        orders = jax.vmap(lambda one_key: jax.random.permutation(one_key, BYTE_DEV - 1))(cut_keys)
        chosen = (jnp.arange(BYTE_DEV - 1, dtype=jnp.int32)[None, :] < counts[:, None] - 1).astype(jnp.int32)
        marks = jnp.zeros((N_SEQ, BYTE_DEV), jnp.int32)
        marks = marks.at[shard_ids[:, None], orders + 1].set(chosen)
        marks = marks.at[:, 0].set(1)
        return jnp.nonzero(marks.reshape(-1), size=NPS)[0].astype(jnp.int32)
    seq_keys = jax.random.split(key, SEQS)
    return jax.vmap(one_sequence)(seq_keys)


def level_of(own_key, shape, cuts, low, top_value):
    gain, own = 1.0, jax.random.fold_in(own_key, 6)
    for dim, blocks in cuts:
        heights = jnp.exp(jax.random.uniform(jax.random.fold_in(own, dim), (blocks,), jnp.float32, low / len(cuts), top_value / len(cuts)))
        gain = gain * jnp.repeat(heights, shape[dim] // blocks).reshape([-1 if axis == dim else 1 for axis in range(len(shape))])
    return gain


def centred(rng, dims, spread, most, cuts=(), kind=jnp.bfloat16):
    values = jax.random.normal(rng, dims, jnp.float32) * spread
    if len(cuts) > 0:
        values = level_of(rng, dims, cuts, -0.22, 0.18) * values
    return jnp.clip(values, min=-most, max=most).astype(kind)


def setup_inputs(seed: int = 0) -> dict:
    key_list = jax.random.split(jax.random.key(seed), 12)
    patch_states = centred(key_list[0], (SEQS, NPS, D), 1.0, 6.0, ((0, 4), (1, 2), (2, 4)))
    residual_grad = centred(key_list[1], (SEQS, NPS, D), 0.5, 3.0, ((0, 4), (1, 2), (2, 4)))
    upstream_value = centred(key_list[2], (SEQS, NPS, KVW), 1.0, 6.0, ((0, 4), (1, 2)))
    norm_gain = jnp.clip(1.0 + 0.18 * jax.random.normal(key_list[3], (D,), jnp.float32), 0.099609375, 1.8984375).astype(jnp.bfloat16)
    value_weight = centred(key_list[4], (KVW, D), D ** -0.5, 0.09375, ((0, 8), (1, 4)))
    out_weight = centred(key_list[5], (DLW, D), DLW ** -0.5, 0.25, ((0, 8), (1, 4)))
    attn_out = centred(key_list[6], (SEQS, NPS, DLW), 1.0, 6.0, ((0, 4), (1, 2)))
    queries = jnp.clip(jax.random.uniform(key_list[7], (SEQS, NPS, DLW), jnp.float32, -1.5, 1.5) * level_of(key_list[7], (SEQS, NPS, DLW), ((0, 4), (1, 2), (2, 4)), -0.4, 0.0), -1.5, 1.5).astype(jnp.bfloat16)
    byte_keys = jnp.clip(jax.random.uniform(key_list[8], (SEQS, SEQ_LEN, DLW), jnp.float32, -1.5, 1.5) * level_of(key_list[8], (SEQS, SEQ_LEN, DLW), ((0, 4), (1, 2), (2, 4)), -0.4, 0.0), -1.5, 1.5).astype(jnp.bfloat16)
    byte_values = centred(key_list[9], (SEQS, SEQ_LEN, DLW), 1.0, 6.0, ((0, 4), (1, 2), (2, 4)))
    patch_starts = draw_patch_starts(jax.random.fold_in(key_list[11], 71), 0)
    return dict(patch_states=patch_states, residual_grad=residual_grad, upstream_value=upstream_value, norm_gain=norm_gain, value_weight=value_weight, out_weight=out_weight, attn_out=attn_out, queries=queries, byte_keys=byte_keys, byte_values=byte_values, patch_starts=patch_starts)


def cross_backward(query_rows, grad_rows, keys, values, segment_ids, count):
    nbytes = keys.shape[0]
    heads = keys.shape[1] // HD
    scale = 1.0 / math.sqrt(HD)
    query_f = query_rows.astype(jnp.float32).reshape(nbytes, heads, HD)
    grad_f = grad_rows.astype(jnp.float32).reshape(nbytes, heads, HD)
    keys_f = keys.astype(jnp.float32).reshape(nbytes, heads, HD)
    values_f = values.astype(jnp.float32).reshape(nbytes, heads, HD)
    scores = lax.optimization_barrier(jnp.sum(query_f * keys_f, axis=-1)) * scale
    expo = jnp.exp(scores)
    totals = jax.ops.segment_sum(expo, segment_ids, num_segments=count)
    probs = expo / totals[segment_ids]
    grad_values = (probs[..., None] * grad_f).reshape(nbytes, heads * HD).astype(jnp.bfloat16)
    prob_grad = lax.optimization_barrier(jnp.sum(grad_f * values_f, axis=-1))
    mass = jax.ops.segment_sum(probs * prob_grad, segment_ids, num_segments=count)
    score_grad = probs * (prob_grad - mass[segment_ids])
    grad_keys = (score_grad[..., None] * query_f * scale).reshape(nbytes, heads * HD).astype(jnp.bfloat16)
    return (grad_keys, grad_values)

def reference(patch_states, residual_grad, upstream_value, norm_gain, value_weight, out_weight, attn_out, queries, byte_keys, byte_values, patch_starts):
    states32 = patch_states.reshape(-1, D).astype(jnp.float32)
    gain32 = norm_gain.astype(jnp.float32)
    inv_rms = lax.rsqrt(lax.optimization_barrier(jnp.mean(states32 * states32, axis=1)) + 1e-05)
    normed = (states32 * inv_rms[:, None] * gain32).astype(jnp.bfloat16)
    upstream = upstream_value.reshape(-1, KVW)
    grad_normed = jnp.dot(upstream, value_weight, preferred_element_type=jnp.float32)
    wgrad_value = lax.dot_general(upstream, normed, (((0,), (0,)), ((), ())), preferred_element_type=jnp.float32)
    cross_sum = lax.optimization_barrier(jnp.sum(grad_normed * gain32 * states32, axis=1))
    grad_patch = (residual_grad.reshape(-1, D).astype(jnp.float32) + inv_rms[:, None] * gain32 * grad_normed - (inv_rms ** 3)[:, None] * states32 * (cross_sum / D)[:, None]).astype(jnp.bfloat16)
    wgrad_out = lax.dot_general(attn_out.reshape(-1, DLW), grad_patch, (((0,), (0,)), ((), ())), preferred_element_type=jnp.float32)
    grad_attn = lax.dot_general(grad_patch, out_weight, (((1,), (1,)), ((), ())), preferred_element_type=jnp.float32)
    grad_attn = grad_attn.astype(jnp.bfloat16).reshape(SEQS, NPS, DLW)

    def one_sequence(item):
        starts, grad_rows, query_rows, keys, values = item
        positions = jnp.arange(SEQ_LEN, dtype=jnp.int32)
        patch_index = (jnp.searchsorted(starts, positions, side='right') - 1).astype(jnp.int32)
        return cross_backward(query_rows[patch_index], grad_rows[patch_index], keys, values, patch_index, NPS)
    grad_keys, grad_values = lax.map(one_sequence, (patch_starts, grad_attn, queries, byte_keys, byte_values))
    return (wgrad_value, wgrad_out, grad_keys, grad_values)
```

```python
import functools
import math

import jax
import jax.numpy as jnp
from jax import lax
from jax.experimental import pallas as pl
from jax.experimental.pallas import tpu as pltpu
from jax.sharding import PartitionSpec as P

HD = 128


def member_sum(member32, terms):
    return lax.dot_general(
        member32,
        terms,
        (((0,), (0,)), ((), ())),
        precision=lax.Precision.HIGHEST,
        preferred_element_type=jnp.float32,
    )


def member_spread(member32, totals):
    return jnp.dot(
        member32, totals, precision=lax.Precision.HIGHEST, preferred_element_type=jnp.float32
    )


def cross_backward(member, segment_rows, keys, values, head_width):
    nbytes = keys.shape[0]
    heads = keys.shape[1] // HD
    scale = 1.0 / math.sqrt(HD)
    member32 = member.astype(jnp.float32)
    picked = jnp.dot(member, segment_rows, preferred_element_type=jnp.float32).astype(jnp.bfloat16)
    grad_f = picked[:, :head_width].astype(jnp.float32).reshape(nbytes, heads, HD)
    query_f = picked[:, head_width:].astype(jnp.float32).reshape(nbytes, heads, HD)
    keys_f = keys.astype(jnp.float32).reshape(nbytes, heads, HD)
    values_f = values.astype(jnp.float32).reshape(nbytes, heads, HD)
    scores = jnp.sum(query_f * keys_f, axis=-1) * scale
    expo = jnp.exp(scores)
    totals = member_spread(member32, member_sum(member32, expo))
    probs = expo / totals
    grad_values = (probs[..., None] * grad_f).reshape(nbytes, heads * HD).astype(jnp.bfloat16)
    prob_grad = jnp.sum(grad_f * values_f, axis=-1)
    mass = member_spread(member32, member_sum(member32, probs * prob_grad))
    score_grad = probs * (prob_grad - mass)
    grad_keys = (
        (score_grad[..., None] * query_f * scale).reshape(nbytes, heads * HD).astype(jnp.bfloat16)
    )
    return (grad_keys, grad_values)


def contract_rows(left, right):
    return lax.dot_general(
        left, right, (((0,), (0,)), ((), ())), preferred_element_type=jnp.float32
    )


def on_device(
    patch_states,
    residual_grad,
    upstream_value,
    norm_gain,
    value_weight,
    out_weight,
    attn_out,
    queries,
    byte_keys,
    byte_values,
    patch_starts,
):
    states = patch_states[0]
    patches = states.shape[0]
    width_local = states.shape[1]
    model_width = width_local * lax.axis_size("tensor")
    states32 = states.astype(jnp.float32)
    gain32 = norm_gain.astype(jnp.float32)
    upstream = upstream_value[0]
    context = attn_out[0]
    value_full, out_full = (
        lax.all_gather(value_weight, ("dp", "seq"), axis=0, tiled=True),
        lax.all_gather(out_weight, ("dp", "seq"), axis=0, tiled=True),
    )
    grad_normed = jnp.dot(upstream, value_full, preferred_element_type=jnp.float32)
    square_part = jnp.sum(states32 * states32, axis=1)
    cross_part = jnp.sum(grad_normed * gain32 * states32, axis=1)
    square_sum, cross_sum = lax.psum((square_part, cross_part), "tensor")
    inv_rms = lax.rsqrt(square_sum / model_width + 1e-05)
    normed = (states32 * inv_rms[:, None] * gain32).astype(jnp.bfloat16)
    grad_patch = (
        residual_grad[0].astype(jnp.float32)
        + inv_rms[:, None] * gain32 * grad_normed
        - (inv_rms**3)[:, None] * states32 * (cross_sum / model_width)[:, None]
    ).astype(jnp.bfloat16)
    partial_attn = lax.dot_general(
        grad_patch, out_full, (((1,), (1,)), ((), ())), preferred_element_type=jnp.float32
    )
    columns = upstream
    wgrad_value = lax.psum_scatter(
        contract_rows(columns, normed), ("dp", "seq"), scatter_dimension=0, tiled=True
    )
    columns = context
    wgrad_out = lax.psum_scatter(
        contract_rows(columns, grad_patch), ("dp", "seq"), scatter_dimension=0, tiled=True
    )
    attn_all = lax.psum(partial_attn, "tensor").astype(jnp.bfloat16)
    head_width = queries.shape[2]
    grad_attn = lax.dynamic_slice_in_dim(
        attn_all, lax.axis_index("tensor") * head_width, head_width, 1
    )
    starts = patch_starts[0]
    total_patches = starts.shape[0]
    seq_count = lax.axis_size("seq")
    seq_pos = lax.axis_index("seq")
    byte_count = byte_keys.shape[1]
    window_len = 2 * patches
    owners = starts // byte_count
    shard_ids = jnp.arange(seq_count, dtype=jnp.int32)
    firsts = jnp.sum((owners[None, :] < shard_ids[:, None]).astype(jnp.int32), axis=1)
    my_first = jnp.sum(firsts * (shard_ids == seq_pos).astype(jnp.int32))
    payload = jnp.concatenate([grad_attn, queries[0]], axis=1)
    padded_starts = jnp.concatenate(
        [starts, jnp.full((window_len,), 2 * total_patches * byte_count + byte_count, jnp.int32)]
    )
    local_starts = lax.dynamic_slice_in_dim(padded_starts, my_first, window_len)
    positions = seq_pos * byte_count + jnp.arange(byte_count, dtype=jnp.int32)
    reached = local_starts[None, :] <= positions[:, None]
    after = jnp.concatenate([reached[:, 1:], jnp.zeros((byte_count, 1), bool)], axis=1)
    member = (reached & jnp.logical_not(after)).astype(jnp.bfloat16)
    mine = seq_pos * patches + jnp.arange(patches, dtype=jnp.int32)
    targets = lax.dynamic_slice_in_dim(owners, seq_pos * patches, patches)
    target_first = jnp.sum((owners[None, :] < targets[:, None]).astype(jnp.int32), axis=1)
    slots = mine - jnp.maximum(seq_pos * patches, target_first)
    dest = targets * patches + slots
    place = (jnp.arange(seq_count * patches, dtype=jnp.int32)[:, None] == dest[None, :]).astype(
        jnp.bfloat16
    )
    outgoing = jnp.dot(place, payload, preferred_element_type=jnp.float32).astype(jnp.bfloat16)
    outgoing = outgoing.reshape(seq_count, patches, 2 * head_width)
    incoming = lax.all_to_all(outgoing, "seq", split_axis=0, concat_axis=0, tiled=True)
    wanted = my_first + jnp.arange(window_len, dtype=jnp.int32)
    sources = wanted // patches
    received_row = sources * patches + wanted - jnp.maximum(sources * patches, my_first)
    select = (
        received_row[:, None] == jnp.arange(seq_count * patches, dtype=jnp.int32)[None, :]
    ).astype(jnp.bfloat16)
    segment_rows = jnp.dot(
        select,
        incoming.reshape(seq_count * patches, 2 * head_width),
        preferred_element_type=jnp.float32,
    ).astype(jnp.bfloat16)
    grad_keys, grad_values = cross_backward(
        member, segment_rows, byte_keys[0], byte_values[0], head_width
    )
    return (wgrad_value, wgrad_out, grad_keys[None], grad_values[None])


def split3(x):
    hi = x.astype(jnp.bfloat16).astype(jnp.float32)
    rest = x - hi
    mid = rest.astype(jnp.bfloat16).astype(jnp.float32)
    return hi, mid, rest - mid


def byte_kernel(
    block, scale, bounds, rows, keys, values, gk, gv, member, picked, expo, pgrad, sums, table
):
    phase = pl.program_id(0)
    step = pl.program_id(1)
    here = pl.ds(pl.multiple_of(step * block, block), block)
    width = bounds.shape[1]
    lane = lax.broadcasted_iota(jnp.int32, (block, 128), 1)

    @pl.when((phase == 0) & (step == 0))
    def _():
        sums[...] = jnp.zeros_like(sums)

    @pl.when(phase == 0)
    def _():
        pos = step * block + lax.broadcasted_iota(jnp.int32, (block, width), 0)
        inside = (bounds[0:1, :] <= pos) & (bounds[1:2, :] > pos)
        mem = jnp.where(inside, 1.0, 0.0).astype(jnp.bfloat16)
        member[here, :] = mem
        rows_b = jnp.dot(mem, rows[...], preferred_element_type=jnp.float32)
        picked[here, :] = rows_b.astype(jnp.bfloat16)
        score = jnp.sum(rows_b[:, HD:] * keys[...].astype(jnp.float32), axis=1, keepdims=True)
        e = jnp.exp(score * scale)
        pg = jnp.sum(rows_b[:, :HD] * values[...].astype(jnp.float32), axis=1, keepdims=True)
        expo[here, :] = e
        pgrad[here, :] = pg
        cols = jnp.zeros((block, 128), jnp.float32)
        for i, part in enumerate(split3(e) + split3(e * pg)):
            cols = jnp.where(lane == i, part, cols)
        cols_t = cols.T[:16].astype(jnp.bfloat16)
        sums[...] += jnp.dot(cols_t, mem, preferred_element_type=jnp.float32)

    @pl.when((phase == 1) & (step == 0))
    def _():
        total = sums[0:1, :] + sums[1:2, :] + sums[2:3, :]
        inv = jnp.where(total > 0.0, 1.0 / jnp.where(total > 0.0, total, 1.0), 0.0)
        mass = (sums[3:4, :] + sums[4:5, :] + sums[5:6, :]) * inv
        row = lax.broadcasted_iota(jnp.int32, (128, width), 0)
        tab = jnp.zeros((128, width), jnp.float32)
        for i, part in enumerate(split3(inv) + split3(mass)):
            tab = jnp.where(row == i, part, tab)
        table[...] = tab.astype(jnp.bfloat16)

    @pl.when(phase == 1)
    def _():
        spread = lax.dot_general(
            member[here, :],
            table[...],
            (((1,), (1,)), ((), ())),
            preferred_element_type=jnp.float32,
        )
        inv = jnp.sum(jnp.where(lane < 3, spread, 0.0), axis=1, keepdims=True)
        mass = jnp.sum(jnp.where((lane >= 3) & (lane < 6), spread, 0.0), axis=1, keepdims=True)
        probs = expo[here, :] * inv
        sg = probs * (pgrad[here, :] - mass) * scale
        both = picked[here, :].astype(jnp.float32)
        gv[...] = (probs * both[:, :HD]).astype(jnp.bfloat16)
        gk[...] = (sg * both[:, HD:]).astype(jnp.bfloat16)


def byte_backward(bounds, rows, keys, values):
    nbytes = keys.shape[0]
    width = rows.shape[0]
    block = 512
    steps = nbytes // block
    shape = jax.ShapeDtypeStruct(keys.shape, jnp.bfloat16)
    return pl.pallas_call(
        functools.partial(byte_kernel, block, 1.0 / math.sqrt(HD)),
        grid=(2, steps),
        out_shape=(shape, shape),
        in_specs=[
            pl.BlockSpec((2, width), lambda p, i: (0, 0)),
            pl.BlockSpec((width, 2 * HD), lambda p, i: (0, 0)),
            pl.BlockSpec((block, HD), lambda p, i: (i * (1 - p) + (steps - 1) * p, 0)),
            pl.BlockSpec((block, HD), lambda p, i: (i * (1 - p) + (steps - 1) * p, 0)),
        ],
        out_specs=[
            pl.BlockSpec((block, HD), lambda p, i: (i * p, 0)),
            pl.BlockSpec((block, HD), lambda p, i: (i * p, 0)),
        ],
        scratch_shapes=[
            pltpu.VMEM((nbytes, width), jnp.bfloat16),
            pltpu.VMEM((nbytes, 2 * HD), jnp.bfloat16),
            pltpu.VMEM((nbytes, 1), jnp.float32),
            pltpu.VMEM((nbytes, 1), jnp.float32),
            pltpu.VMEM((16, width), jnp.float32),
            pltpu.VMEM((128, width), jnp.bfloat16),
        ],
        compiler_params=pltpu.CompilerParams(vmem_limit_bytes=56 * 1024 * 1024),
    )(bounds, rows, keys, values)


def patch_kernel(
    ndp, nt, states, resid, up, gain, vw, ow, ctx, q, wgv, wgo, pay,
    wall, sqs, sqr, part, ws, yr, zs, zr, pas, par, gn, nrm, gpat, trans, gsend, grecv, qrecv,
    s_az, r_az, s_ay, r_ay, s_sq, r_sq, s_ry, r_ry, s_rz, r_rz, s_pa, r_pa, s_g, r_g,
):
    dp, sq, tn = lax.axis_index("dp"), lax.axis_index("seq"), lax.axis_index("tensor")
    patches, width = states.shape
    model = width * nt
    mine = dp * 2 + sq
    tall = 128
    nrow = patches // tall
    ncol = width // 256

    def zdev(k):
        return (lax.rem(dp + k, ndp), sq, tn)

    def tdev(k):
        return (dp, sq, lax.rem(tn + k, nt))

    ydev = (dp, 1 - sq, tn)

    def copy(src, dst, ssem, rsem, dev):
        return pltpu.make_async_remote_copy(
            src_ref=src, dst_ref=dst, send_sem=ssem, recv_sem=rsem,
            device_id=dev, device_id_type=pl.DeviceIdType.MESH,
        )

    barrier = pltpu.get_barrier_semaphore()
    peers = [zdev(k) for k in range(1, ndp)] + [tdev(k) for k in range(1, nt)] + [ydev]
    for dev in peers:
        pl.semaphore_signal(barrier, inc=1, device_id=dev, device_id_type=pl.DeviceIdType.MESH)
    pl.semaphore_wait(barrier, len(peers))

    sent = []

    def go(c):
        c.start()
        sent.append(c)
        return c

    weights = (vw, ow)

    def gather_start(w):
        z = [
            go(copy(weights[w], wall.at[w, mine], s_az.at[w, k - 1], r_az.at[w, k - 1], zdev(k)))
            for k in range(1, ndp)
        ]
        y = [go(copy(weights[w], wall.at[w, mine], s_ay.at[w, 0], r_ay.at[w, 0], ydev))]
        return z, y

    def gather_forward(w, z, y):
        for k in range(1, ndp):
            z[k - 1].wait_recv()
            slot = lax.rem(dp + (ndp - k), ndp) * 2 + sq
            y.append(
                go(copy(wall.at[w, slot], wall.at[w, slot], s_ay.at[w, k], r_ay.at[w, k], ydev))
            )

    vz, vy = gather_start(0)
    qc = go(copy(q, qrecv, s_g.at[0], r_g.at[0], ydev))

    def row_loop(fn):
        def body(i, _):
            fn(pl.ds(pl.multiple_of(i * tall, tall), tall), i)
            return 0

        lax.fori_loop(0, nrow, body, 0)

    def to_row(col):
        return jnp.broadcast_to(col, (tall, 128)).T[:8]

    def total_of(which):
        rows = sqs[which] + sqr[which, 0]
        for k in range(1, nt - 1):
            rows = rows + sqr[which, k]
        return rows

    def share(which):
        return [
            go(copy(sqs.at[which], sqr.at[which, k - 1], s_sq.at[which, k - 1],
                    r_sq.at[which, k - 1], tdev(k)))
            for k in range(1, nt)
        ]

    def column(rows):
        return jnp.broadcast_to(rows[0:1, :], (128, patches)).T

    def square(here, i):
        x = states[here, :].astype(jnp.float32)
        sqs[0, i] = to_row(jnp.sum(x * x, axis=1, keepdims=True))

    row_loop(square)
    sq_copies = share(0)
    oz, oy = gather_start(1)
    wall[0, mine] = vw[...]
    wall[1, mine] = ow[...]
    gather_forward(0, vz, vy)
    for c in sq_copies:
        c.wait_recv()

    def inverse(i):
        rows = sqs[0, i]
        for k in range(nt - 1):
            rows = rows + sqr[0, k, i]
        col = jnp.broadcast_to(rows[0:1, :], (128, tall)).T[:, 0:1]
        return lax.rsqrt(col / model + 1e-05)

    def normalise(here, i):
        x = states[here, :].astype(jnp.float32)
        nrm[here, :] = (x * inverse(i) * gain[...].astype(jnp.float32)).astype(jnp.bfloat16)

    row_loop(normalise)

    def wgrad(w, left, right):
        trans[...] = left[...].T
        nblk, rows_per = part.shape[1], part.shape[2]

        def body(c, _):
            cols = pl.ds(pl.multiple_of(c * 256, 256), 256)
            out = jnp.dot(trans[...], right[:, cols], preferred_element_type=jnp.float32)
            part[w, :, :, cols] = out.reshape(nblk, rows_per, 256)
            return 0

        lax.fori_loop(0, ncol, body, 0)
        copies = []
        for j in range(ndp):
            ws[w, j] = part[w, j * 2 + (1 - sq)].astype(jnp.bfloat16)
            copies.append(go(copy(ws.at[w, j], yr.at[w, j], s_ry.at[w, j], r_ry.at[w, j], ydev)))
        return copies

    def wgrad_forward(w, copies):
        for c in copies:
            c.wait_recv()
        out = []
        for k in range(1, ndp):
            t = lax.rem(dp + k, ndp)
            zs[w, k - 1] = (part[w, t * 2 + sq] + yr[w, t].astype(jnp.float32)).astype(jnp.bfloat16)
            out.append(
                go(copy(zs.at[w, k - 1], zr.at[w, k - 1], s_rz.at[w, k - 1], r_rz.at[w, k - 1],
                        zdev(k)))
            )
        return out

    def wgrad_finish(w, copies, dst):
        total = part[w, mine] + yr[w, dp].astype(jnp.float32)
        for k, c in enumerate(copies):
            c.wait_recv()
            total = total + zr[w, k].astype(jnp.float32)
        dst[...] = total

    wv_y = wgrad(0, up, nrm)
    for c in vy:
        c.wait_recv()

    def project(here, i):
        full = wall[0].reshape(up.shape[1], width)
        g = jnp.dot(up[here, :], full, preferred_element_type=jnp.float32)
        gn[here, :] = g
        x = states[here, :].astype(jnp.float32)
        cross = g * gain[...].astype(jnp.float32) * x
        sqs[1, i] = to_row(jnp.sum(cross, axis=1, keepdims=True))

    row_loop(project)
    cr_copies = share(1)
    gather_forward(1, oz, oy)
    wv_z = wgrad_forward(0, wv_y)
    for c in cr_copies:
        c.wait_recv()

    def make_grad(here, i):
        inv = inverse(i)
        rows = sqs[1, i]
        for k in range(nt - 1):
            rows = rows + sqr[1, k, i]
        cross = jnp.broadcast_to(rows[0:1, :], (128, tall)).T[:, 0:1] / model
        x = states[here, :].astype(jnp.float32)
        gpat[here, :] = (
            resid[here, :].astype(jnp.float32)
            + inv * gain[...].astype(jnp.float32) * gn[here, :]
            - (inv * inv * inv * cross) * x
        ).astype(jnp.bfloat16)

    row_loop(make_grad)
    for c in oy:
        c.wait_recv()

    def attn(here, i):
        full = wall[1].reshape(up.shape[1], width)
        p = lax.dot_general(
            gpat[here, :], full, (((1,), (1,)), ((), ())), preferred_element_type=jnp.float32
        )
        for j in range(nt):
            pas[j, here, :] = p[:, j * HD : (j + 1) * HD]

    row_loop(attn)
    for k in range(1, nt):
        ws_slot = lax.rem(tn + k, nt)
        gsend[k] = pas[ws_slot].astype(jnp.bfloat16)
    pa_copies = [
        go(copy(gsend.at[k], par.at[k - 1], s_pa.at[k - 1], r_pa.at[k - 1], tdev(k)))
        for k in range(1, nt)
    ]
    wo_y = wgrad(1, ctx, gpat)
    total = pas[tn]
    for k, c in enumerate(pa_copies):
        c.wait_recv()
        total = total + par[k].astype(jnp.float32)
    gsend[0] = total.astype(jnp.bfloat16)
    gc = go(copy(gsend.at[0], grecv, s_g.at[1], r_g.at[1], ydev))
    wo_z = wgrad_forward(1, wo_y)
    wgrad_finish(0, wv_z, wgv)
    pay[sq, :, :HD] = gsend[0]
    pay[sq, :, HD:] = q[...]
    qc.wait_recv()
    gc.wait_recv()
    pay[1 - sq, :, :HD] = grecv[...]
    pay[1 - sq, :, HD:] = qrecv[...]
    wgrad_finish(1, wo_z, wgo)
    for c in sent:
        c.wait_send()


def patch_backward(ndp, nt, states, resid, up, gain, vw, ow, ctx, q):
    patches, width = states.shape
    rows = vw.shape[0]
    nblk = 2 * ndp
    bf, f32 = jnp.bfloat16, jnp.float32
    nrow = patches // 128
    vmem = pl.BlockSpec(memory_space=pltpu.VMEM)
    dma = pltpu.SemaphoreType.DMA
    return pl.pallas_call(
        functools.partial(patch_kernel, ndp, nt),
        out_shape=(
            jax.ShapeDtypeStruct((rows, width), f32),
            jax.ShapeDtypeStruct((rows, width), f32),
            jax.ShapeDtypeStruct((2, patches, 2 * HD), bf),
        ),
        in_specs=[vmem] * 8,
        out_specs=[vmem] * 3,
        scratch_shapes=[
            pltpu.VMEM((2, nblk, rows, width), bf),
            pltpu.VMEM((2, nrow, 8, 128), f32),
            pltpu.VMEM((2, nt - 1, nrow, 8, 128), f32),
            pltpu.VMEM((2, nblk, rows, width), f32),
            pltpu.VMEM((2, ndp, rows, width), bf),
            pltpu.VMEM((2, ndp, rows, width), bf),
            pltpu.VMEM((2, ndp - 1, rows, width), bf),
            pltpu.VMEM((2, ndp - 1, rows, width), bf),
            pltpu.VMEM((nt, patches, HD), f32),
            pltpu.VMEM((nt - 1, patches, HD), bf),
            pltpu.VMEM((patches, width), f32),
            pltpu.VMEM((patches, width), bf),
            pltpu.VMEM((patches, width), bf),
            pltpu.VMEM((nblk * rows, patches), bf),
            pltpu.VMEM((nt, patches, HD), bf),
            pltpu.VMEM((patches, HD), bf),
            pltpu.VMEM((patches, HD), bf),
            dma((2, ndp - 1)), dma((2, ndp - 1)),
            dma((2, ndp)), dma((2, ndp)),
            dma((2, nt - 1)), dma((2, nt - 1)),
            dma((2, ndp)), dma((2, ndp)),
            dma((2, ndp - 1)), dma((2, ndp - 1)),
            dma((nt - 1,)), dma((nt - 1,)),
            dma((2,)), dma((2,)),
        ],
        compiler_params=pltpu.CompilerParams(
            collective_id=0, has_side_effects=True, vmem_limit_bytes=56 * 1024 * 1024
        ),
    )(states, resid, up, gain, vw, ow, ctx, q)


def on_device_kernels(
    ndp, nt, patch_states, residual_grad, upstream_value, norm_gain, value_weight, out_weight,
    attn_out, queries, byte_keys, byte_values, patch_starts,
):
    wgv, wgo, pay = patch_backward(
        ndp, nt, patch_states[0], residual_grad[0], upstream_value[0], norm_gain[None],
        value_weight, out_weight, attn_out[0], queries[0],
    )
    byte_count = byte_keys.shape[1]
    starts = patch_starts[0] - lax.axis_index("seq") * byte_count
    after = jnp.concatenate([starts[1:], jnp.full((1,), 2 * byte_count, jnp.int32)])
    rows = pay.reshape(-1, 2 * HD)
    gk, gv = byte_backward(jnp.stack([starts, after]), rows, byte_keys[0], byte_values[0])
    return (wgv, wgo, gk[None], gv[None])


def solution(mesh):
    ndp, nseq, nt = mesh.shape["dp"], mesh.shape["seq"], mesh.shape["tensor"]
    use_kernels = nseq == 2 and ndp <= 4
    body = functools.partial(on_device_kernels, ndp, nt) if use_kernels else on_device
    return jax.shard_map(
        body,
        mesh=mesh,
        in_specs=(
            P("dp", "seq", "tensor"),
            P("dp", "seq", "tensor"),
            P("dp", "seq", None),
            P("tensor"),
            P(("dp", "seq"), "tensor"),
            P(("dp", "seq"), "tensor"),
            P("dp", "seq", None),
            P("dp", "seq", "tensor"),
            P("dp", "seq", "tensor"),
            P("dp", "seq", "tensor"),
            P("dp", None),
        ),
        out_specs=(
            P(("dp", "seq"), "tensor"),
            P(("dp", "seq"), "tensor"),
            P("dp", "seq", "tensor"),
            P("dp", "seq", "tensor"),
        ),
        check_vma=False,
    )
```

```python
import functools
import math

import jax
import jax.numpy as jnp
from jax import lax
from jax.experimental import pallas as pl
from jax.experimental.pallas import tpu as pltpu
from jax.sharding import PartitionSpec as P

HD = 128


def member_sum(member32, terms):
    return lax.dot_general(
        member32,
        terms,
        (((0,), (0,)), ((), ())),
        precision=lax.Precision.HIGHEST,
        preferred_element_type=jnp.float32,
    )


def member_spread(member32, totals):
    return jnp.dot(
        member32, totals, precision=lax.Precision.HIGHEST, preferred_element_type=jnp.float32
    )


def cross_backward(member, segment_rows, keys, values, head_width):
    nbytes = keys.shape[0]
    heads = keys.shape[1] // HD
    scale = 1.0 / math.sqrt(HD)
    member32 = member.astype(jnp.float32)
    picked = jnp.dot(member, segment_rows, preferred_element_type=jnp.float32).astype(jnp.bfloat16)
    grad_f = picked[:, :head_width].astype(jnp.float32).reshape(nbytes, heads, HD)
    query_f = picked[:, head_width:].astype(jnp.float32).reshape(nbytes, heads, HD)
    keys_f = keys.astype(jnp.float32).reshape(nbytes, heads, HD)
    values_f = values.astype(jnp.float32).reshape(nbytes, heads, HD)
    scores = jnp.sum(query_f * keys_f, axis=-1) * scale
    expo = jnp.exp(scores)
    totals = member_spread(member32, member_sum(member32, expo))
    probs = expo / totals
    grad_values = (probs[..., None] * grad_f).reshape(nbytes, heads * HD).astype(jnp.bfloat16)
    prob_grad = jnp.sum(grad_f * values_f, axis=-1)
    mass = member_spread(member32, member_sum(member32, probs * prob_grad))
    score_grad = probs * (prob_grad - mass)
    grad_keys = (
        (score_grad[..., None] * query_f * scale).reshape(nbytes, heads * HD).astype(jnp.bfloat16)
    )
    return (grad_keys, grad_values)


def contract_rows(left, right):
    return lax.dot_general(
        left, right, (((0,), (0,)), ((), ())), preferred_element_type=jnp.float32
    )


def on_device(
    patch_states,
    residual_grad,
    upstream_value,
    norm_gain,
    value_weight,
    out_weight,
    attn_out,
    queries,
    byte_keys,
    byte_values,
    patch_starts,
):
    states = patch_states[0]
    patches = states.shape[0]
    width_local = states.shape[1]
    model_width = width_local * lax.axis_size("tensor")
    states32 = states.astype(jnp.float32)
    gain32 = norm_gain.astype(jnp.float32)
    upstream = upstream_value[0]
    context = attn_out[0]
    value_full, out_full = (
        lax.all_gather(value_weight, ("dp", "seq"), axis=0, tiled=True),
        lax.all_gather(out_weight, ("dp", "seq"), axis=0, tiled=True),
    )
    grad_normed = jnp.dot(upstream, value_full, preferred_element_type=jnp.float32)
    square_part = jnp.sum(states32 * states32, axis=1)
    cross_part = jnp.sum(grad_normed * gain32 * states32, axis=1)
    square_sum, cross_sum = lax.psum((square_part, cross_part), "tensor")
    inv_rms = lax.rsqrt(square_sum / model_width + 1e-05)
    normed = (states32 * inv_rms[:, None] * gain32).astype(jnp.bfloat16)
    grad_patch = (
        residual_grad[0].astype(jnp.float32)
        + inv_rms[:, None] * gain32 * grad_normed
        - (inv_rms**3)[:, None] * states32 * (cross_sum / model_width)[:, None]
    ).astype(jnp.bfloat16)
    partial_attn = lax.dot_general(
        grad_patch, out_full, (((1,), (1,)), ((), ())), preferred_element_type=jnp.float32
    )
    columns = upstream
    wgrad_value = lax.psum_scatter(
        contract_rows(columns, normed), ("dp", "seq"), scatter_dimension=0, tiled=True
    )
    columns = context
    wgrad_out = lax.psum_scatter(
        contract_rows(columns, grad_patch), ("dp", "seq"), scatter_dimension=0, tiled=True
    )
    attn_all = lax.psum(partial_attn, "tensor").astype(jnp.bfloat16)
    head_width = queries.shape[2]
    grad_attn = lax.dynamic_slice_in_dim(
        attn_all, lax.axis_index("tensor") * head_width, head_width, 1
    )
    starts = patch_starts[0]
    total_patches = starts.shape[0]
    seq_count = lax.axis_size("seq")
    seq_pos = lax.axis_index("seq")
    byte_count = byte_keys.shape[1]
    window_len = 2 * patches
    owners = starts // byte_count
    shard_ids = jnp.arange(seq_count, dtype=jnp.int32)
    firsts = jnp.sum((owners[None, :] < shard_ids[:, None]).astype(jnp.int32), axis=1)
    my_first = jnp.sum(firsts * (shard_ids == seq_pos).astype(jnp.int32))
    payload = jnp.concatenate([grad_attn, queries[0]], axis=1)
    padded_starts = jnp.concatenate(
        [starts, jnp.full((window_len,), 2 * total_patches * byte_count + byte_count, jnp.int32)]
    )
    local_starts = lax.dynamic_slice_in_dim(padded_starts, my_first, window_len)
    positions = seq_pos * byte_count + jnp.arange(byte_count, dtype=jnp.int32)
    reached = local_starts[None, :] <= positions[:, None]
    after = jnp.concatenate([reached[:, 1:], jnp.zeros((byte_count, 1), bool)], axis=1)
    member = (reached & jnp.logical_not(after)).astype(jnp.bfloat16)
    mine = seq_pos * patches + jnp.arange(patches, dtype=jnp.int32)
    targets = lax.dynamic_slice_in_dim(owners, seq_pos * patches, patches)
    target_first = jnp.sum((owners[None, :] < targets[:, None]).astype(jnp.int32), axis=1)
    slots = mine - jnp.maximum(seq_pos * patches, target_first)
    dest = targets * patches + slots
    place = (jnp.arange(seq_count * patches, dtype=jnp.int32)[:, None] == dest[None, :]).astype(
        jnp.bfloat16
    )
    outgoing = jnp.dot(place, payload, preferred_element_type=jnp.float32).astype(jnp.bfloat16)
    outgoing = outgoing.reshape(seq_count, patches, 2 * head_width)
    incoming = lax.all_to_all(outgoing, "seq", split_axis=0, concat_axis=0, tiled=True)
    wanted = my_first + jnp.arange(window_len, dtype=jnp.int32)
    sources = wanted // patches
    received_row = sources * patches + wanted - jnp.maximum(sources * patches, my_first)
    select = (
        received_row[:, None] == jnp.arange(seq_count * patches, dtype=jnp.int32)[None, :]
    ).astype(jnp.bfloat16)
    segment_rows = jnp.dot(
        select,
        incoming.reshape(seq_count * patches, 2 * head_width),
        preferred_element_type=jnp.float32,
    ).astype(jnp.bfloat16)
    grad_keys, grad_values = cross_backward(
        member, segment_rows, byte_keys[0], byte_values[0], head_width
    )
    return (wgrad_value, wgrad_out, grad_keys[None], grad_values[None])


def split3(x):
    hi = x.astype(jnp.bfloat16).astype(jnp.float32)
    rest = x - hi
    mid = rest.astype(jnp.bfloat16).astype(jnp.float32)
    return hi, mid, rest - mid


def byte_sums(block, scale, first, last, bounds, rows, keys, values, member, picked, expo, pgrad, sums):
    width = bounds.shape[1]
    lane = lax.broadcasted_iota(jnp.int32, (block, 128), 1)

    def body(step, _):
        here = pl.ds(pl.multiple_of(step * block, block), block)
        pos = step * block + lax.broadcasted_iota(jnp.int32, (block, width), 0)
        inside = (bounds[0:1, :] <= pos) & (bounds[1:2, :] > pos)
        mem = jnp.where(inside, 1.0, 0.0).astype(jnp.bfloat16)
        member[here, :] = mem
        rows_b = jnp.dot(mem, rows[...].reshape(width, 2 * HD), preferred_element_type=jnp.float32)
        picked[here, :] = rows_b.astype(jnp.bfloat16)
        score = jnp.sum(rows_b[:, HD:] * keys[here, :].astype(jnp.float32), axis=1, keepdims=True)
        e = jnp.exp(score * scale)
        pg = jnp.sum(rows_b[:, :HD] * values[here, :].astype(jnp.float32), axis=1, keepdims=True)
        expo[here, :] = e
        pgrad[here, :] = pg
        cols = jnp.zeros((block, 128), jnp.float32)
        for i, part in enumerate(split3(e) + split3(e * pg)):
            cols = jnp.where(lane == i, part, cols)
        cols_t = cols.T[:16].astype(jnp.bfloat16)
        sums[...] += jnp.dot(cols_t, mem, preferred_element_type=jnp.float32)
        return 0

    lax.fori_loop(first, last, body, 0)


def byte_table(sums, table):
    width = sums.shape[1]
    total = sums[0:1, :] + sums[1:2, :] + sums[2:3, :]
    inv = jnp.where(total > 0.0, 1.0 / jnp.where(total > 0.0, total, 1.0), 0.0)
    mass = (sums[3:4, :] + sums[4:5, :] + sums[5:6, :]) * inv
    row = lax.broadcasted_iota(jnp.int32, (128, width), 0)
    tab = jnp.zeros((128, width), jnp.float32)
    for i, part in enumerate(split3(inv) + split3(mass)):
        tab = jnp.where(row == i, part, tab)
    table[...] = tab.astype(jnp.bfloat16)


def byte_grads(block, scale, first, last, member, picked, expo, pgrad, table, gk, gv):
    lane = lax.broadcasted_iota(jnp.int32, (block, 128), 1)

    def body(step, _):
        here = pl.ds(pl.multiple_of(step * block, block), block)
        spread = lax.dot_general(
            member[here, :],
            table[...],
            (((1,), (1,)), ((), ())),
            preferred_element_type=jnp.float32,
        )
        inv = jnp.sum(jnp.where(lane < 3, spread, 0.0), axis=1, keepdims=True)
        mass = jnp.sum(jnp.where((lane >= 3) & (lane < 6), spread, 0.0), axis=1, keepdims=True)
        probs = expo[here, :] * inv
        sg = probs * (pgrad[here, :] - mass) * scale
        both = picked[here, :].astype(jnp.float32)
        gv[here, :] = (probs * both[:, :HD]).astype(jnp.bfloat16)
        gk[here, :] = (sg * both[:, HD:]).astype(jnp.bfloat16)
        return 0

    lax.fori_loop(first, last, body, 0)


def patch_kernel(
    ndp, nt, states, resid, up, gain, vw, ow, ctx, q, bounds, keys_in, values_in,
    wgv, wgo, gk_out, gv_out,
    wall, sqs, sqr, part, ws, yr, zs, zr, pas, par, gn, nrm, gpat, trans, gsend, grecv, qrecv,
    pay, keys, values, member, picked, expo, pgrad, sums, table, s_in, s_out,
    s_az, r_az, s_ay, r_ay, s_sq, r_sq, s_ry, r_ry, s_rz, r_rz, s_pa, r_pa, s_g, r_g,
):
    dp, sq, tn = lax.axis_index("dp"), lax.axis_index("seq"), lax.axis_index("tensor")
    patches, width = states.shape
    model = width * nt
    mine = dp * 2 + sq
    tall = 128
    nrow = patches // tall
    ncol = width // 256

    def zdev(k):
        return (lax.rem(dp + k, ndp), sq, tn)

    def tdev(k):
        return (dp, sq, lax.rem(tn + k, nt))

    ydev = (dp, 1 - sq, tn)

    def copy(src, dst, ssem, rsem, dev):
        return pltpu.make_async_remote_copy(
            src_ref=src, dst_ref=dst, send_sem=ssem, recv_sem=rsem,
            device_id=dev, device_id_type=pl.DeviceIdType.MESH,
        )

    k_in = pltpu.make_async_copy(keys_in, keys, s_in.at[0])
    v_in = pltpu.make_async_copy(values_in, values, s_in.at[1])
    k_in.start()
    v_in.start()

    barrier = pltpu.get_barrier_semaphore()
    peers = [zdev(k) for k in range(1, ndp)] + [tdev(k) for k in range(1, nt)] + [ydev]
    for dev in peers:
        pl.semaphore_signal(barrier, inc=1, device_id=dev, device_id_type=pl.DeviceIdType.MESH)
    pl.semaphore_wait(barrier, len(peers))

    sent = []

    def go(c):
        c.start()
        sent.append(c)
        return c

    weights = (vw, ow)

    def gather_start(w):
        z = [
            go(copy(weights[w], wall.at[w, mine], s_az.at[w, k - 1], r_az.at[w, k - 1], zdev(k)))
            for k in range(1, ndp)
        ]
        y = [go(copy(weights[w], wall.at[w, mine], s_ay.at[w, 0], r_ay.at[w, 0], ydev))]
        return z, y

    def gather_forward(w, z, y):
        for k in range(1, ndp):
            z[k - 1].wait_recv()
            slot = lax.rem(dp + (ndp - k), ndp) * 2 + sq
            y.append(
                go(copy(wall.at[w, slot], wall.at[w, slot], s_ay.at[w, k], r_ay.at[w, k], ydev))
            )

    vz, vy = gather_start(0)
    qc = go(copy(q, qrecv, s_g.at[0], r_g.at[0], ydev))

    def row_loop(fn):
        def body(i, _):
            fn(pl.ds(pl.multiple_of(i * tall, tall), tall), i)
            return 0

        lax.fori_loop(0, nrow, body, 0)

    def to_row(col):
        return jnp.broadcast_to(col, (tall, 128)).T[:8]

    def total_of(which):
        rows = sqs[which] + sqr[which, 0]
        for k in range(1, nt - 1):
            rows = rows + sqr[which, k]
        return rows

    def share(which):
        return [
            go(copy(sqs.at[which], sqr.at[which, k - 1], s_sq.at[which, k - 1],
                    r_sq.at[which, k - 1], tdev(k)))
            for k in range(1, nt)
        ]

    def column(rows):
        return jnp.broadcast_to(rows[0:1, :], (128, patches)).T

    def square(here, i):
        x = states[here, :].astype(jnp.float32)
        sqs[0, i] = to_row(jnp.sum(x * x, axis=1, keepdims=True))

    row_loop(square)
    sq_copies = share(0)
    oz, oy = gather_start(1)
    wall[0, mine] = vw[...]
    wall[1, mine] = ow[...]
    gather_forward(0, vz, vy)
    for c in sq_copies:
        c.wait_recv()

    def inverse(i):
        rows = sqs[0, i]
        for k in range(nt - 1):
            rows = rows + sqr[0, k, i]
        col = jnp.broadcast_to(rows[0:1, :], (128, tall)).T[:, 0:1]
        return lax.rsqrt(col / model + 1e-05)

    def normalise(here, i):
        x = states[here, :].astype(jnp.float32)
        nrm[here, :] = (x * inverse(i) * gain[...].astype(jnp.float32)).astype(jnp.bfloat16)

    row_loop(normalise)

    def wgrad(w, left, right):
        trans[...] = left[...].T
        nblk, rows_per = part.shape[1], part.shape[2]

        def body(c, _):
            cols = pl.ds(pl.multiple_of(c * 256, 256), 256)
            out = jnp.dot(trans[...], right[:, cols], preferred_element_type=jnp.float32)
            part[w, :, :, cols] = out.reshape(nblk, rows_per, 256)
            return 0

        lax.fori_loop(0, ncol, body, 0)
        copies = []
        for j in range(ndp):
            ws[w, j] = part[w, j * 2 + (1 - sq)].astype(jnp.bfloat16)
            copies.append(go(copy(ws.at[w, j], yr.at[w, j], s_ry.at[w, j], r_ry.at[w, j], ydev)))
        return copies

    def wgrad_forward(w, copies):
        for c in copies:
            c.wait_recv()
        out = []
        for k in range(1, ndp):
            t = lax.rem(dp + k, ndp)
            zs[w, k - 1] = (part[w, t * 2 + sq] + yr[w, t].astype(jnp.float32)).astype(jnp.bfloat16)
            out.append(
                go(copy(zs.at[w, k - 1], zr.at[w, k - 1], s_rz.at[w, k - 1], r_rz.at[w, k - 1],
                        zdev(k)))
            )
        return out

    def wgrad_finish(w, copies, dst):
        total = part[w, mine] + yr[w, dp].astype(jnp.float32)
        for k, c in enumerate(copies):
            c.wait_recv()
            total = total + zr[w, k].astype(jnp.float32)
        dst[...] = total

    for c in vy:
        c.wait_recv()

    def project(here, i):
        full = wall[0].reshape(up.shape[1], width)
        g = jnp.dot(up[here, :], full, preferred_element_type=jnp.float32)
        gn[here, :] = g
        x = states[here, :].astype(jnp.float32)
        cross = g * gain[...].astype(jnp.float32) * x
        sqs[1, i] = to_row(jnp.sum(cross, axis=1, keepdims=True))

    row_loop(project)
    cr_copies = share(1)
    gather_forward(1, oz, oy)
    for c in cr_copies:
        c.wait_recv()

    def make_grad(here, i):
        inv = inverse(i)
        rows = sqs[1, i]
        for k in range(nt - 1):
            rows = rows + sqr[1, k, i]
        cross = jnp.broadcast_to(rows[0:1, :], (128, tall)).T[:, 0:1] / model
        x = states[here, :].astype(jnp.float32)
        gpat[here, :] = (
            resid[here, :].astype(jnp.float32)
            + inv * gain[...].astype(jnp.float32) * gn[here, :]
            - (inv * inv * inv * cross) * x
        ).astype(jnp.bfloat16)

    row_loop(make_grad)
    for c in oy:
        c.wait_recv()

    def attn(here, i):
        full = wall[1].reshape(up.shape[1], width)
        p = lax.dot_general(
            gpat[here, :], full, (((1,), (1,)), ((), ())), preferred_element_type=jnp.float32
        )
        for j in range(nt):
            pas[j, here, :] = p[:, j * HD : (j + 1) * HD]

    row_loop(attn)
    for k in range(1, nt):
        ws_slot = lax.rem(tn + k, nt)
        gsend[k] = pas[ws_slot].astype(jnp.bfloat16)
    pa_copies = [
        go(copy(gsend.at[k], par.at[k - 1], s_pa.at[k - 1], r_pa.at[k - 1], tdev(k)))
        for k in range(1, nt)
    ]
    wv_y = wgrad(0, up, nrm)
    total = pas[tn]
    for k, c in enumerate(pa_copies):
        c.wait_recv()
        total = total + par[k].astype(jnp.float32)
    gsend[0] = total.astype(jnp.bfloat16)
    gc = go(copy(gsend.at[0], grecv, s_g.at[1], r_g.at[1], ydev))
    wo_y = wgrad(1, ctx, gpat)
    sums[...] = jnp.zeros_like(sums)
    pay[sq, :, :HD] = gsend[0]
    pay[sq, :, HD:] = q[...]
    k_in.wait()
    v_in.wait()
    qc.wait_recv()
    gc.wait_recv()
    pay[1 - sq, :, :HD] = grecv[...]
    pay[1 - sq, :, HD:] = qrecv[...]
    block = 512
    steps = keys.shape[0] // block
    scale = 1.0 / math.sqrt(HD)
    args = (bounds, pay, keys, values, member, picked, expo, pgrad, sums)
    byte_sums(block, scale, 0, steps // 4, *args)
    wv_z = wgrad_forward(0, wv_y)
    byte_sums(block, scale, steps // 4, 3 * steps // 4, *args)
    wo_z = wgrad_forward(1, wo_y)
    byte_sums(block, scale, 3 * steps // 4, steps, *args)
    byte_table(sums, table)
    byte_grads(block, scale, 0, steps, member, picked, expo, pgrad, table, keys, values)
    k_out = pltpu.make_async_copy(keys, gk_out, s_out.at[0])
    v_out = pltpu.make_async_copy(values, gv_out, s_out.at[1])
    k_out.start()
    v_out.start()
    wgrad_finish(0, wv_z, wgv)
    wgrad_finish(1, wo_z, wgo)
    k_out.wait()
    v_out.wait()
    for c in sent:
        c.wait_send()


def patch_backward(ndp, nt, states, resid, up, gain, vw, ow, ctx, q, bounds, keys, values):
    patches, width = states.shape
    rows = vw.shape[0]
    nblk = 2 * ndp
    nbytes = keys.shape[0]
    bf, f32 = jnp.bfloat16, jnp.float32
    nrow = patches // 128
    vmem = pl.BlockSpec(memory_space=pltpu.VMEM)
    dma = pltpu.SemaphoreType.DMA
    return pl.pallas_call(
        functools.partial(patch_kernel, ndp, nt),
        out_shape=(
            jax.ShapeDtypeStruct((rows, width), f32),
            jax.ShapeDtypeStruct((rows, width), f32),
            jax.ShapeDtypeStruct(keys.shape, bf),
            jax.ShapeDtypeStruct(keys.shape, bf),
        ),
        in_specs=[vmem] * 9 + [pl.BlockSpec(memory_space=pl.ANY)] * 2,
        out_specs=[vmem] * 2 + [pl.BlockSpec(memory_space=pl.ANY)] * 2,
        scratch_shapes=[
            pltpu.VMEM((2, nblk, rows, width), bf),
            pltpu.VMEM((2, nrow, 8, 128), f32),
            pltpu.VMEM((2, nt - 1, nrow, 8, 128), f32),
            pltpu.VMEM((2, nblk, rows, width), f32),
            pltpu.VMEM((2, ndp, rows, width), bf),
            pltpu.VMEM((2, ndp, rows, width), bf),
            pltpu.VMEM((2, ndp - 1, rows, width), bf),
            pltpu.VMEM((2, ndp - 1, rows, width), bf),
            pltpu.VMEM((nt, patches, HD), f32),
            pltpu.VMEM((nt - 1, patches, HD), bf),
            pltpu.VMEM((patches, width), f32),
            pltpu.VMEM((patches, width), bf),
            pltpu.VMEM((patches, width), bf),
            pltpu.VMEM((nblk * rows, patches), bf),
            pltpu.VMEM((nt, patches, HD), bf),
            pltpu.VMEM((patches, HD), bf),
            pltpu.VMEM((patches, HD), bf),
            pltpu.VMEM((2, patches, 2 * HD), bf),
            pltpu.VMEM(keys.shape, bf),
            pltpu.VMEM(keys.shape, bf),
            pltpu.VMEM((nbytes, 2 * patches), bf),
            pltpu.VMEM((nbytes, 2 * HD), bf),
            pltpu.VMEM((nbytes, 1), f32),
            pltpu.VMEM((nbytes, 1), f32),
            pltpu.VMEM((16, 2 * patches), f32),
            pltpu.VMEM((128, 2 * patches), bf),
            dma((2,)), dma((2,)),
            dma((2, ndp - 1)), dma((2, ndp - 1)),
            dma((2, ndp)), dma((2, ndp)),
            dma((2, nt - 1)), dma((2, nt - 1)),
            dma((2, ndp)), dma((2, ndp)),
            dma((2, ndp - 1)), dma((2, ndp - 1)),
            dma((nt - 1,)), dma((nt - 1,)),
            dma((2,)), dma((2,)),
        ],
        compiler_params=pltpu.CompilerParams(
            collective_id=0, has_side_effects=True, vmem_limit_bytes=62 * 1024 * 1024
        ),
    )(states, resid, up, gain, vw, ow, ctx, q, bounds, keys, values)


def on_device_kernels(
    ndp, nt, patch_states, residual_grad, upstream_value, norm_gain, value_weight, out_weight,
    attn_out, queries, byte_keys, byte_values, patch_starts,
):
    byte_count = byte_keys.shape[1]
    starts = patch_starts[0] - lax.axis_index("seq") * byte_count
    after = jnp.concatenate([starts[1:], jnp.full((1,), 2 * byte_count, jnp.int32)])
    wgv, wgo, gk, gv = patch_backward(
        ndp, nt, patch_states[0], residual_grad[0], upstream_value[0], norm_gain[None],
        value_weight, out_weight, attn_out[0], queries[0],
        jnp.stack([starts, after]), byte_keys[0], byte_values[0],
    )
    return (wgv, wgo, gk[None], gv[None])


def solution(mesh):
    ndp, nseq, nt = mesh.shape["dp"], mesh.shape["seq"], mesh.shape["tensor"]
    use_kernels = nseq == 2 and ndp <= 4
    body = functools.partial(on_device_kernels, ndp, nt) if use_kernels else on_device
    return jax.shard_map(
        body,
        mesh=mesh,
        in_specs=(
            P("dp", "seq", "tensor"),
            P("dp", "seq", "tensor"),
            P("dp", "seq", None),
            P("tensor"),
            P(("dp", "seq"), "tensor"),
            P(("dp", "seq"), "tensor"),
            P("dp", "seq", None),
            P("dp", "seq", "tensor"),
            P("dp", "seq", "tensor"),
            P("dp", "seq", "tensor"),
            P("dp", None),
        ),
        out_specs=(
            P(("dp", "seq"), "tensor"),
            P(("dp", "seq"), "tensor"),
            P("dp", "seq", "tensor"),
            P("dp", "seq", "tensor"),
        ),
        check_vma=False,
    )
```
